32 devices in a mesh: facet: 4 (over y, x), band: 4 (over z), sub: 2 (over core).
Axes of the slice: x: 2, y: 2, z: 4, core: 2. Of those that a mesh axis runs over, the one named last changes fastest.
Arguments:
- facets: bfloat16 [8192, 2048], P(('facet', 'band')), may hold values from -6 to 6
- window: float32 [2048], replicated, may hold values from 0.5 to 1.5
- facet_offsets: int32 [4, 2], replicated, may hold values from 0 to 49151
- row_offsets: int32 [8], replicated, may hold values from 0 to 49151
- column_offset: int32 [1], replicated, may hold values from 0 to 49151
- kernel: bfloat16 [256, 256], replicated, may hold values from -0.375 to 0.375
- tile_counts: int32 [8, 16, 16], replicated, may hold values from 0 to 32
Outputs:
- residual: bfloat16 [8192, 2048], P(('facet', 'band'))
The draws below stay inside these ranges and needn't reach their ends.
All inputs are finite; a program needn't handle non-finite values.
Results may differ from the reference program's by a relative error of at most 0.013.
Values may be sent and summed in bfloat16 or wider, within the bound.
A program may use at most 64 MiB of HBM per device.

```python
import math
import jax
import jax.numpy as jnp
from jax import lax

IMAGE = 49152
FACET = 2048
CONTRIB = 256
TILE = 16
FACETS = 4
SUBGRIDS = 8


def with_ends(array, stream_key, least, largest):
    extent = array.shape
    spot = [jax.random.randint(jax.random.fold_in(stream_key, axis), (), 0, extent[axis]) for axis in range(len(extent))]
    array = array.at[tuple(spot)].set(least)
    longest = extent.index(max(extent))
    spot[longest] = (spot[longest] + 1) % extent[longest]
    return array.at[tuple(spot)].set(largest)


def levels(key, dims, shards, least, top_value):
    loudness = 1.0
    for dim, parts in shards:
        draws = jax.random.uniform(jax.random.fold_in(jax.random.fold_in(key, 6), dim), (parts,), jnp.float32, least / len(shards), top_value / len(shards))
        loudness = loudness * jnp.repeat(jnp.exp(draws), dims[dim] // parts).reshape((-1,) + (1,) * (len(dims) - 1 - dim))
    return loudness


def scatter_about(rng, shape, scale, reach, cuts=(), held_as=jnp.bfloat16):
    array = jax.random.normal(rng, shape, jnp.float32) * scale
    if len(cuts) > 0:
        array = levels(rng, shape, cuts, -0.22, 0.18) * array
    return jnp.clip(array, min=-reach, max=reach).astype(held_as)


def setup_inputs(seed: int = 0) -> dict:
    splits = jax.random.split(jax.random.key(seed), 8)
    facets = scatter_about(splits[0], (FACETS * FACET, FACET), 1.0, 6.0, ((0, 16),))
    window = jnp.clip(jax.random.uniform(splits[1], (FACET,), jnp.float32, 0.5, 1.5), 0.5, 1.5)
    facet_offsets = with_ends(jax.random.randint(splits[2], (FACETS, 2), 0, IMAGE), jax.random.fold_in(splits[2], 1), 0, IMAGE - 1).astype(jnp.int32)
    row_offsets = with_ends(jax.random.randint(splits[3], (SUBGRIDS,), 0, IMAGE), jax.random.fold_in(splits[3], 1), 0, IMAGE - 1).astype(jnp.int32)
    column_offset = jax.random.randint(splits[4], (1,), 0, IMAGE).astype(jnp.int32)
    kernel = scatter_about(splits[5], (CONTRIB, CONTRIB), CONTRIB ** -0.5, 0.375)
    tile_counts = with_ends(jax.random.randint(splits[6], (SUBGRIDS, CONTRIB // TILE, CONTRIB // TILE), 0, 33), jax.random.fold_in(splits[6], 1), 0, 32).astype(jnp.int32)
    return {"facets": facets, "window": window, "facet_offsets": facet_offsets, "row_offsets": row_offsets, "column_offset": column_offset, "kernel": kernel, "tile_counts": tile_counts}


def modular_product(first, second):
    upper_bits = first // 256
    lower_bits = first % 256
    reduced = upper_bits * second % IMAGE
    reduced = reduced * 256 % IMAGE
    return (reduced + lower_bits * second) % IMAGE

def phase_table(frequency, position):
    reduced = modular_product(frequency % IMAGE, position % IMAGE)
    angle = reduced.astype(jnp.float32) * (2.0 * math.pi / IMAGE)
    return (jnp.cos(angle), jnp.sin(angle))

def matmul(left, right):
    return jnp.dot(left.astype(jnp.float32), right.astype(jnp.float32), precision=lax.Precision.HIGHEST)

def einsum_exact(form, left, right):
    return jnp.einsum(form, left.astype(jnp.float32), right.astype(jnp.float32), precision=lax.Precision.HIGHEST)

def reference(facets, window, facet_offsets, row_offsets, column_offset, kernel, tile_counts):
    cells = jnp.arange(FACET, dtype=jnp.int32)
    frequencies = jnp.arange(CONTRIB, dtype=jnp.int32)
    row_freqs = (row_offsets[:, None] + frequencies[None, :]).reshape(SUBGRIDS * CONTRIB)
    a_scale = 1.0 / math.sqrt(FACET * FACETS)
    b_scale = 1.0 / math.sqrt(FACET)
    back_scale = 1.0 / math.sqrt(SUBGRIDS * CONTRIB)
    out_scale = 1.0 / math.sqrt(CONTRIB)
    images = facets.reshape(FACETS, FACET, FACET)

    def column_tables(offset_y):
        return phase_table(column_offset[0] + frequencies[:, None], offset_y + cells[None, :])

    def forward(total, item):
        image, offset = item
        cosine, sine = column_tables(offset[1])
        col_real = (cosine * window[None, :] * b_scale).astype(jnp.bfloat16)
        col_imag = (-sine * window[None, :] * b_scale).astype(jnp.bfloat16)
        t_real = matmul(image, col_real.T).astype(jnp.bfloat16)
        t_imag = matmul(image, col_imag.T).astype(jnp.bfloat16)
        row_cos, row_sin = phase_table(row_freqs[:, None], offset[0] + cells[None, :])
        a_real = (row_cos * a_scale).astype(jnp.bfloat16)
        a_imag = (-row_sin * a_scale).astype(jnp.bfloat16)
        part_real = matmul(a_real, t_real) - matmul(a_imag, t_imag)
        part_imag = matmul(a_real, t_imag) + matmul(a_imag, t_real)
        return (total + jnp.stack([part_real, part_imag]), None)
    start_total = jnp.zeros((2, SUBGRIDS * CONTRIB, CONTRIB), jnp.float32)
    summed, _ = lax.scan(forward, start_total, (images, facet_offsets))
    grids = summed.reshape(2, SUBGRIDS, CONTRIB, CONTRIB).astype(jnp.bfloat16)
    tiles = CONTRIB // TILE
    counts = tile_counts.astype(jnp.float32)
    ratio = counts / (counts + 4.0)
    weights = jnp.broadcast_to(ratio[:, :, None, :, None], (SUBGRIDS, tiles, TILE, tiles, TILE))
    weights = weights.reshape(SUBGRIDS, CONTRIB, CONTRIB)
    y_grid = einsum_exact('csij,kj->csik', grids, kernel).astype(jnp.bfloat16)
    z_grid = einsum_exact('ki,csil->cskl', kernel, y_grid)
    w_grid = (weights[None] * z_grid).astype(jnp.bfloat16)
    u_grid = einsum_exact('jk,csjl->cskl', kernel, w_grid).astype(jnp.bfloat16)
    r_grid = einsum_exact('csij,jl->csil', u_grid, kernel).astype(jnp.bfloat16)
    stacked = r_grid.reshape(2, SUBGRIDS * CONTRIB, CONTRIB)

    def backward(offset):
        row_cos, row_sin = phase_table(row_freqs[:, None], offset[0] + cells[None, :])
        back_real = (row_cos * back_scale).astype(jnp.bfloat16)
        back_imag = (row_sin * back_scale).astype(jnp.bfloat16)
        e_real = matmul(back_real.T, stacked[0]) - matmul(back_imag.T, stacked[1])
        e_imag = matmul(back_real.T, stacked[1]) + matmul(back_imag.T, stacked[0])
        cosine, sine = column_tables(offset[1])
        out_cos = (cosine * out_scale).astype(jnp.bfloat16)
        out_sin = (sine * out_scale).astype(jnp.bfloat16)
        image = matmul(e_real.astype(jnp.bfloat16), out_cos) - matmul(e_imag.astype(jnp.bfloat16), out_sin)
        return (window[None, :] * image).astype(jnp.bfloat16)
    result = lax.map(backward, facet_offsets)
    return result.reshape(FACETS * FACET, FACET)
```

```python
import functools
import math

import jax
import jax.numpy as jnp
from jax import lax
from jax.experimental import pallas as pl
from jax.experimental.pallas import tpu as pltpu
from jax.sharding import PartitionSpec as P

IMAGE = 49152
QUARTER = IMAGE // 4
LANES = 128
FINE = 32
F32 = jnp.float32
BF16 = jnp.bfloat16
I32 = jnp.int32


def wrap(value):
    return value - float(IMAGE) * jnp.floor(value * (1.0 / IMAGE))


def phase_pair(first, second):
    upper = (first >> 8).astype(F32)
    lower = (first & 255).astype(F32)
    other = second.astype(F32)
    reduced = wrap(wrap(upper * other) * 256.0)
    reduced = wrap(reduced + lower * other)
    turn = jnp.floor(reduced * (1.0 / QUARTER) + 0.5)
    angle = (reduced - turn * float(QUARTER)) * (2.0 * math.pi / IMAGE)
    square = angle * angle
    sine = 1.0 / 120 + square * (-1.0 / 5040 + square * (1.0 / 362880))
    sine = angle + angle * square * (-1.0 / 6 + square * sine)
    cosine = -1.0 / 720 + square * (1.0 / 40320 + square * (-1.0 / 3628800))
    cosine = 1.0 + square * (-0.5 + square * (1.0 / 24 + square * cosine))
    quadrant = turn.astype(I32)
    odd = (quadrant & 1) == 1
    real = jnp.where(odd, sine, cosine)
    imag = jnp.where(odd, cosine, sine)
    real = jnp.where(((quadrant + 1) & 2) != 0, -real, real)
    imag = jnp.where((quadrant & 2) != 0, -imag, imag)
    return real, imag


def iota(shape, dim):
    return lax.broadcasted_iota(I32, shape, dim)


def nt(left, right):
    return lax.dot_general(left, right, (((1,), (1,)), ((), ())), preferred_element_type=F32)


def nn(left, right):
    return jnp.dot(left, right, preferred_element_type=F32)


def column_tables(column, offset, contrib, width, store):
    shape = (contrib, LANES)
    freq = column + iota(shape, 0)
    lane = iota(shape, 1)
    coarse_c, coarse_s = phase_pair(freq, offset + LANES * lane)
    fine_c, fine_s = phase_pair(freq, lane)
    for at in range(width // LANES):
        c = coarse_c[:, at : at + 1]
        s = coarse_s[:, at : at + 1]
        store(at, c * fine_c - s * fine_s, s * fine_c + c * fine_s)


def row_tables(start, offset, rows, contrib, store):
    coarse = rows // FINE
    cc, cs = phase_pair(
        start + iota((coarse, contrib), 1), offset + FINE * iota((coarse, contrib), 0)
    )
    fc, fs = phase_pair(start + iota((FINE, contrib), 1), iota((FINE, contrib), 0))
    for at in range(coarse):
        c = cc[at : at + 1, :]
        s = cs[at : at + 1, :]
        store(at * FINE, (c * fc - s * fs).astype(BF16), (s * fc + c * fs).astype(BF16))


def forward_kernel(offsets, starts, column, facets, window, out, cols, left, rows_tab):
    facet_at = lax.axis_index("facet")
    band_at = lax.axis_index("band")
    sub_at = lax.axis_index("sub")
    facet_count, band_count, piece, contrib = out.shape
    rows, width = facets.shape
    b_scale = 1.0 / math.sqrt(width)
    a_scale = 1.0 / math.sqrt(width * facet_count)

    def store_col(at, cosine, sine):
        here = slice(at * LANES, (at + 1) * LANES)
        taper = window[:, here]
        cols[0:contrib, here] = (cosine * taper).astype(BF16)
        cols[contrib:, here] = (sine * taper).astype(BF16)

    column_tables(column[0], offsets[facet_at, 1], contrib, width, store_col)
    t = nt(cols[...], facets[...]) * b_scale
    t_real = t[:contrib].astype(BF16)
    t_imag = (-t[contrib:]).astype(BF16)
    left[:contrib, :rows] = t_real
    left[:contrib, rows:] = t_imag
    left[contrib:, :rows] = t_imag
    left[contrib:, rows:] = -t_real
    position = offsets[facet_at, 0] + band_at * rows

    def step(g, carry):
        def store_row(at, cosine, sine):
            rows_tab[at : at + FINE, :] = cosine
            rows_tab[rows + at : rows + at + FINE, :] = sine

        row_tables(starts[sub_at * band_count + g], position, rows, contrib, store_row)
        part = nn(left[...], rows_tab[...]) * a_scale
        for f in range(facet_count):
            out[f, g] = part[f * piece : (f + 1) * piece].astype(BF16)
        return carry

    lax.fori_loop(0, band_count, step, 0)


def exchange_kernel(
    parts, kernel, kernel_t, counts, out,
    recv1, own2, recv2, planes,
    s1, r1, s2, r2, s3, r3, s4, r4, s5, r5, s6, r6,
):
    facet_at = lax.axis_index("facet")
    band_at = lax.axis_index("band")
    sub_at = lax.axis_index("sub")
    facet_count, band_count, piece, contrib = parts.shape
    sub_count = out.shape[0]
    half = facet_count // 2
    group = (facet_at // half) * half
    member = facet_at % half

    def remote(src, dst, send, recv, **where):
        return pltpu.make_async_remote_copy(
            src_ref=src, dst_ref=dst, send_sem=send, recv_sem=recv,
            device_id=where, device_id_type=pl.DeviceIdType.MESH,
        )

    barrier = pltpu.get_barrier_semaphore()
    for d in range(1, facet_count):
        pl.semaphore_signal(barrier, 1, device_id={"facet": lax.rem(facet_at + d, facet_count)},
                            device_id_type=pl.DeviceIdType.MESH)
    for d in range(1, band_count):
        pl.semaphore_signal(barrier, 1, device_id={"band": lax.rem(band_at + d, band_count)},
                            device_id_type=pl.DeviceIdType.MESH)
    for d in range(1, sub_count):
        pl.semaphore_signal(barrier, 1, device_id={"sub": lax.rem(sub_at + d, sub_count)},
                            device_id_type=pl.DeviceIdType.MESH)
    pl.semaphore_wait(barrier, facet_count + band_count + sub_count - 3)

    first = {}
    for e in range(band_count):
        g = lax.rem(band_at + 1 + e, band_count)
        for d in range(1, facet_count):
            peer = lax.rem(facet_at + d, facet_count)
            copy = remote(parts.at[peer, g], recv1.at[d - 1, g], s1.at[d - 1, e],
                          r1.at[d - 1, g], facet=peer)
            copy.start()
            first[d, e] = copy
    second = {}
    total = None
    for e in range(band_count):
        g = lax.rem(band_at + 1 + e, band_count)
        total = parts[facet_at, g].astype(F32)
        for d in range(1, facet_count):
            remote(parts.at[0, 0], recv1.at[d - 1, g], s1.at[d - 1, e], r1.at[d - 1, g],
                   facet=facet_at).wait_recv()
            total = total + recv1[d - 1, g].astype(F32)
        if e < band_count - 1:
            own2[e] = total.astype(BF16)
            copy = remote(own2.at[e], recv2.at[e], s2.at[e], r2.at[e], band=g)
            copy.start()
            second[e] = copy
    for e in range(band_count - 1):
        second[e].wait_recv()
        total = total + recv2[e].astype(F32)
    planes[member] = total.astype(BF16)
    third = {}
    for d in range(1, half):
        peer = group + lax.rem(member + d, half)
        copy = remote(planes.at[member], planes.at[member], s3.at[d - 1], r3.at[d - 1], facet=peer)
        copy.start()
        third[d] = copy
    tiles = counts.shape[1]
    side = contrib // tiles
    spread = (iota((contrib, tiles), 0) // side == iota((contrib, tiles), 1)).astype(BF16)
    mine = counts[sub_at * band_count + band_at].astype(F32).astype(BF16)
    seen = nt(nt(spread, mine).astype(BF16), spread)
    weight = seen / (seen + 4.0)
    for d in range(1, half):
        third[d].wait_recv()
    grid = planes[...].astype(F32).reshape(contrib, contrib).astype(BF16)
    y = nn(kernel[...], grid).astype(BF16)
    z = nt(y, kernel[...])
    w = (weight * z).astype(BF16)
    u = nn(w, kernel[...]).astype(BF16)
    first_row = pl.multiple_of(member * piece, piece)
    result = nn(kernel_t[pl.ds(first_row, piece), :], u)
    out[sub_at, band_at, facet_at] = result.astype(BF16)
    last = []

    def fan(b, f, to_facets):
        ref = out.at[sub_at, b, f]
        if to_facets:
            for d in range(1, facet_count):
                copy = remote(ref, ref, s5.at[d - 1, b], r5.at[d - 1, b],
                              facet=lax.rem(facet_at + d, facet_count))
                copy.start()
                last.append(copy)
        for d in range(1, sub_count):
            copy = remote(ref, ref, s6.at[d - 1, b, f], r6.at[d - 1, b, f],
                          sub=lax.rem(sub_at + d, sub_count))
            copy.start()
            last.append(copy)

    fourth = []
    for d in range(1, band_count):
        ref = out.at[sub_at, band_at, facet_at]
        copy = remote(ref, ref, s4.at[d - 1], r4.at[d - 1],
                      band=lax.rem(band_at + d, band_count))
        copy.start()
        fourth.append(copy)
    fan(band_at, facet_at, True)
    order = [d for pair in zip(range(1, band_count), range(band_count - 1, 0, -1)) for d in pair]
    order = list(dict.fromkeys(order))
    for d in order:
        b = lax.rem(band_at + band_count - d, band_count)
        ref = out.at[sub_at, b, facet_at]
        remote(ref, ref, s4.at[d - 1], r4.at[d - 1], band=b).wait_recv()
        fan(b, facet_at, True)
    for e in [0] + order:
        b = lax.rem(band_at + band_count - e, band_count)
        for d in range(1, facet_count):
            f = lax.rem(facet_at + facet_count - d, facet_count)
            ref = out.at[sub_at, b, f]
            remote(ref, ref, s5.at[d - 1, b], r5.at[d - 1, b], facet=f).wait_recv()
            fan(b, f, False)
    for d in range(1, sub_count):
        other = lax.rem(sub_at + d, sub_count)
        for b in range(band_count):
            for f in range(facet_count):
                ref = out.at[other, b, f]
                remote(ref, ref, s6.at[d - 1, b, f], r6.at[d - 1, b, f], sub=other).wait_recv()
    for copy in list(first.values()) + list(second.values()) + list(third.values()) + fourth + last:
        copy.wait_send()


def backward_kernel(offsets, starts, column, window, grids, out, cols, cos_tab, sin_tab, joined):
    facet_at = lax.axis_index("facet")
    band_at = lax.axis_index("band")
    sub_count, band_count, facet_count, piece, contrib = grids.shape
    rows, width = out.shape
    back_scale = 1.0 / math.sqrt(sub_count * band_count * contrib)
    out_scale = 1.0 / math.sqrt(contrib)
    position = offsets[facet_at, 0] + band_at * rows

    def step(s, carry):
        here = pl.ds(pl.multiple_of(s * contrib, contrib), contrib)

        def store_row(at, cosine, sine):
            cos_tab[at : at + FINE, here] = cosine
            sin_tab[at : at + FINE, here] = sine

        row_tables(starts[s], position, rows, contrib, store_row)
        block = grids[s // band_count, s % band_count].astype(F32)
        joined[:, here] = block.reshape(facet_count * piece, contrib).astype(BF16)
        return carry

    lax.fori_loop(0, sub_count * band_count, step, 0)

    def store_col(at, cosine, sine):
        here = slice(at * LANES, (at + 1) * LANES)
        cols[0:contrib, here] = cosine.astype(BF16)
        cols[contrib:, here] = sine.astype(BF16)

    column_tables(column[0], offsets[facet_at, 1], contrib, width, store_col)
    by_cos = nt(cos_tab[...], joined[...])
    by_sin = nt(sin_tab[...], joined[...])
    real = (by_cos[:, :contrib] - by_sin[:, contrib:]) * back_scale
    imag = (by_cos[:, contrib:] + by_sin[:, :contrib]) * back_scale
    both = jnp.concatenate([real.astype(BF16), (-imag).astype(BF16)], axis=1)
    step_width = min(width, 512)
    for at in range(width // step_width):
        here = slice(at * step_width, (at + 1) * step_width)
        image = nn(both, cols[:, here])
        out[:, here] = (window[:, here] * out_scale * image).astype(BF16)


def body(sizes, facets, window, facet_offsets, row_offsets, column_offset, kernel, tile_counts):
    facet_count, band_count, sub_count = sizes
    rows, width = facets.shape
    contrib = kernel.shape[0]
    subgrids = row_offsets.shape[0]
    piece = 2 * contrib // facet_count
    half = facet_count // 2
    smem = pl.BlockSpec(memory_space=pltpu.SMEM)
    vmem = pl.BlockSpec(memory_space=pltpu.VMEM)
    taper = window.reshape(1, width)
    parts = pl.pallas_call(
        forward_kernel,
        out_shape=jax.ShapeDtypeStruct((facet_count, band_count, piece, contrib), BF16),
        in_specs=[smem, smem, smem, vmem, vmem],
        out_specs=vmem,
        scratch_shapes=[
            pltpu.VMEM((2 * contrib, width), BF16),
            pltpu.VMEM((2 * contrib, 2 * rows), BF16),
            pltpu.VMEM((2 * rows, contrib), BF16),
        ],
        name="forward",
    )(facet_offsets, row_offsets, column_offset, facets, taper)
    dma = pltpu.SemaphoreType.DMA
    shapes = [
        (facet_count - 1, band_count),
        (band_count - 1,),
        (max(half - 1, 1),),
        (band_count - 1,),
        (facet_count - 1, band_count),
        (max(sub_count - 1, 1), band_count, facet_count),
    ]
    grids = pl.pallas_call(
        exchange_kernel,
        out_shape=jax.ShapeDtypeStruct((sub_count, band_count, facet_count, piece, contrib), BF16),
        in_specs=[vmem] * 4,
        out_specs=vmem,
        scratch_shapes=[
            pltpu.VMEM((facet_count - 1, band_count, piece, contrib), BF16),
            pltpu.VMEM((band_count - 1, piece, contrib), BF16),
            pltpu.VMEM((band_count - 1, piece, contrib), BF16),
            pltpu.VMEM((half, piece, contrib), BF16),
        ]
        + [dma(shape) for shape in shapes for _ in range(2)],
        compiler_params=pltpu.CompilerParams(collective_id=0, has_side_effects=True),
        name="exchange",
    )(parts, kernel, kernel.T, tile_counts)
    return pl.pallas_call(
        backward_kernel,
        out_shape=jax.ShapeDtypeStruct((rows, width), BF16),
        in_specs=[smem, smem, smem, vmem, vmem],
        out_specs=vmem,
        scratch_shapes=[
            pltpu.VMEM((2 * contrib, width), BF16),
            pltpu.VMEM((rows, subgrids * contrib), BF16),
            pltpu.VMEM((rows, subgrids * contrib), BF16),
            pltpu.VMEM((2 * contrib, subgrids * contrib), BF16),
        ],
        name="backward",
    )(facet_offsets, row_offsets, column_offset, taper, grids)


def solution(mesh):
    sizes = tuple(mesh.shape[axis] for axis in ("facet", "band", "sub"))
    in_specs = (P(("facet", "band"), None), P(), P(), P(), P(), P(), P())
    out_specs = P(("facet", "band"), None)
    return jax.shard_map(
        functools.partial(body, sizes), mesh=mesh, in_specs=in_specs, out_specs=out_specs, check_vma=False
    )
```

```python
import functools
import math

import jax
import jax.numpy as jnp
from jax import lax
from jax.experimental import pallas as pl
from jax.experimental.pallas import tpu as pltpu
from jax.sharding import PartitionSpec as P

IMAGE = 49152
QUARTER = IMAGE // 4
LANES = 128
FINE = 32
F32 = jnp.float32
BF16 = jnp.bfloat16
I32 = jnp.int32


def wrap(value):
    return value - float(IMAGE) * jnp.floor(value * (1.0 / IMAGE))


def phase_pair(first, second):
    upper = (first >> 8).astype(F32)
    lower = (first & 255).astype(F32)
    other = second.astype(F32)
    reduced = wrap(wrap(upper * other) * 256.0)
    reduced = wrap(reduced + lower * other)
    turn = jnp.floor(reduced * (1.0 / QUARTER) + 0.5)
    angle = (reduced - turn * float(QUARTER)) * (2.0 * math.pi / IMAGE)
    square = angle * angle
    sine = 1.0 / 120 + square * (-1.0 / 5040 + square * (1.0 / 362880))
    sine = angle + angle * square * (-1.0 / 6 + square * sine)
    cosine = -1.0 / 720 + square * (1.0 / 40320 + square * (-1.0 / 3628800))
    cosine = 1.0 + square * (-0.5 + square * (1.0 / 24 + square * cosine))
    quadrant = turn.astype(I32)
    odd = (quadrant & 1) == 1
    real = jnp.where(odd, sine, cosine)
    imag = jnp.where(odd, cosine, sine)
    real = jnp.where(((quadrant + 1) & 2) != 0, -real, real)
    imag = jnp.where((quadrant & 2) != 0, -imag, imag)
    return real, imag


def iota(shape, dim):
    return lax.broadcasted_iota(I32, shape, dim)


def nt(left, right):
    return lax.dot_general(left, right, (((1,), (1,)), ((), ())), preferred_element_type=F32)


def nn(left, right):
    return jnp.dot(left, right, preferred_element_type=F32)


def column_tables(column, offset, contrib, width, store):
    shape = (contrib, LANES)
    freq = column + iota(shape, 0)
    lane = iota(shape, 1)
    coarse_c, coarse_s = phase_pair(freq, offset + LANES * lane)
    fine_c, fine_s = phase_pair(freq, lane)
    for at in range(width // LANES):
        c = coarse_c[:, at : at + 1]
        s = coarse_s[:, at : at + 1]
        store(at, c * fine_c - s * fine_s, s * fine_c + c * fine_s)


def row_tables(start, offset, rows, contrib, store):
    coarse = rows // FINE
    cc, cs = phase_pair(
        start + iota((coarse, contrib), 1), offset + FINE * iota((coarse, contrib), 0)
    )
    fc, fs = phase_pair(start + iota((FINE, contrib), 1), iota((FINE, contrib), 0))
    for at in range(coarse):
        c = cc[at : at + 1, :]
        s = cs[at : at + 1, :]
        store(at * FINE, (c * fc - s * fs).astype(BF16), (s * fc + c * fs).astype(BF16))


def flat(block):
    pieces, rows, contrib = block.shape
    if rows % 16:
        return block.astype(F32).reshape(pieces * rows, contrib).astype(BF16)
    return block.reshape(pieces * rows, contrib)


def exchange_kernel(
    offsets, starts, column, facets_hbm, taper, kernel, counts,
    out, table_hbm,
    facets, cols, left, cos_tab, sin_tab, out_cols, kernel_t, parts,
    recv_a, recv_b, recv_c, recv_d, mid_a, mid_d, own2, recv2, planes, grids, by_cos, by_sin,
    load_sem, table_sem,
    sa, ra, sb, rb, sc, rc, sd, rd, s2, r2, s3, r3, s4, r4, slo, shi, r5, s6, r6,
):
    facet_at = lax.axis_index("facet")
    band_at = lax.axis_index("band")
    sub_at = lax.axis_index("sub")
    band_count, facet_count, piece, contrib = parts.shape
    sub_count = grids.shape[0]
    rows, width = facets.shape
    highs = facet_count // 2
    high = facet_at // 2
    low = facet_at % 2
    beside = high * 2 + (1 - low)
    group = (facet_at // highs) * highs
    member = facet_at % highs
    b_scale = 1.0 / math.sqrt(width)
    a_scale = 1.0 / math.sqrt(width * facet_count)
    back_scale = 1.0 / math.sqrt(sub_count * band_count * contrib)
    started = []

    def remote(src, dst, send, recv, **where):
        return pltpu.make_async_remote_copy(
            src_ref=src, dst_ref=dst, send_sem=send, recv_sem=recv,
            device_id=where, device_id_type=pl.DeviceIdType.MESH,
        )

    def send(*args, **where):
        copy = remote(*args, **where)
        copy.start()
        started.append(copy)

    def across(d):
        return lax.rem(high + d, highs)

    load = pltpu.make_async_copy(facets_hbm, facets, load_sem)
    load.start()
    barrier = pltpu.get_barrier_semaphore()
    for axis, at, count in (
        ("facet", facet_at, facet_count), ("band", band_at, band_count), ("sub", sub_at, sub_count)
    ):
        for d in range(1, count):
            pl.semaphore_signal(barrier, 1, device_id={axis: lax.rem(at + d, count)},
                                device_id_type=pl.DeviceIdType.MESH)

    def store_taper(at, cosine, sine):
        here = slice(at * LANES, (at + 1) * LANES)
        cols[0:contrib, here] = (cosine * taper[:, here]).astype(BF16)
        cols[contrib:, here] = (sine * taper[:, here]).astype(BF16)

    def store_plain(at, cosine, sine):
        here = slice(at * LANES, (at + 1) * LANES)
        out_cols[0:contrib, here] = cosine.astype(BF16)
        out_cols[contrib:, here] = sine.astype(BF16)

    offset_y = offsets[1, facet_at]
    position = offsets[0, facet_at] + band_at * rows

    def make_rows(s):
        def store_row(at, cosine, sine):
            cos_tab[s, at : at + FINE, :] = cosine
            sin_tab[s, at : at + FINE, :] = sine

        row_tables(starts[s], position, rows, contrib, store_row)

    column_tables(column[0], offset_y, contrib, width, store_taper)
    load.wait()
    t = nt(cols[...], facets[...]) * b_scale
    t_real = t[:contrib].astype(BF16)
    t_imag = (-t[contrib:]).astype(BF16)
    left[:contrib, :rows] = t_real
    left[:contrib, rows:] = t_imag
    left[contrib:, :rows] = t_imag
    left[contrib:, rows:] = -t_real

    def owner(e):
        return lax.rem(band_at + 1 + e, band_count)

    for e in range(band_count):
        g = owner(e)
        s = sub_at * band_count + g
        make_rows(s)
        part = (nn(left[:, :rows], cos_tab[s]) + nn(left[:, rows:], sin_tab[s])) * a_scale
        for f in range(facet_count):
            parts[g, f] = part[f * piece : (f + 1) * piece].astype(BF16)
        if e == 0:
            pl.semaphore_wait(barrier, facet_count + band_count + sub_count - 3)
        if e % 2 == 0:
            for h in range(highs):
                send(parts.at[g, 2 * h + 1 - low], recv_a.at[e, h], sa.at[e, h], ra.at[e, h],
                     facet=beside)
        else:
            for d in range(1, highs):
                send(parts.at[g, pl.ds(2 * across(d), 2)], recv_c.at[e, d - 1], sc.at[e, d - 1],
                     rc.at[e, d - 1], facet=2 * across(d) + low)
    for d in range(1, sub_count):
        def other_rows(b, carry, d=d):
            make_rows(lax.rem(sub_at + d, sub_count) * band_count + b)
            return carry

        lax.fori_loop(0, band_count, other_rows, 0)

    def second_hop(e):
        g = owner(e)
        if e % 2 == 0:
            for h in range(highs):
                remote(parts.at[g, 0], recv_a.at[e, h], sa.at[e, h], ra.at[e, h],
                       facet=beside).wait_recv()
            for d in range(1, highs):
                h = across(d)
                mine = parts[g, 2 * h + low].astype(F32) + recv_a[e, h].astype(F32)
                mid_a[e, d - 1] = mine.astype(BF16)
                send(mid_a.at[e, d - 1], recv_b.at[e, d - 1], sb.at[e, d - 1], rb.at[e, d - 1],
                     facet=2 * h + low)
        else:
            mine = parts[g, beside].astype(F32)
            for d in range(1, highs):
                remote(parts.at[g, pl.ds(0, 2)], recv_c.at[e, d - 1], sc.at[e, d - 1],
                       rc.at[e, d - 1], facet=beside).wait_recv()
                mine = mine + recv_c[e, d - 1, 1 - low].astype(F32)
            mid_d[e] = mine.astype(BF16)
            send(mid_d.at[e], recv_d.at[e], sd.at[e], rd.at[e], facet=beside)

    def facet_sum(e):
        g = owner(e)
        total = parts[g, facet_at].astype(F32)
        if e % 2 == 0:
            total = total + recv_a[e, high].astype(F32)
            for d in range(1, highs):
                remote(mid_a.at[e, d - 1], recv_b.at[e, d - 1], sb.at[e, d - 1], rb.at[e, d - 1],
                       facet=beside).wait_recv()
                total = total + recv_b[e, d - 1].astype(F32)
        else:
            for d in range(1, highs):
                total = total + recv_c[e, d - 1, low].astype(F32)
            remote(mid_d.at[e], recv_d.at[e], sd.at[e], rd.at[e], facet=beside).wait_recv()
            total = total + recv_d[e].astype(F32)
        if e < band_count - 1:
            own2[e] = total.astype(BF16)
            send(own2.at[e], recv2.at[e], s2.at[e], r2.at[e], band=g)
        return total

    second_hop(0)
    for e in range(1, band_count):
        second_hop(e)
        facet_sum(e - 1)
    kernel_t[...] = kernel[...].T
    tiles = counts.shape[1]
    side = contrib // tiles
    spread = (iota((contrib, tiles), 0) // side == iota((contrib, tiles), 1)).astype(BF16)
    tile = counts[sub_at * band_count + band_at].astype(F32).astype(BF16)
    seen = nt(nt(spread, tile).astype(BF16), spread)
    weight = seen / (seen + 4.0)
    total = facet_sum(band_count - 1)
    for e in range(band_count - 1):
        remote(own2.at[e], recv2.at[e], s2.at[e], r2.at[e], band=band_at).wait_recv()
        total = total + recv2[e].astype(F32)
    planes[member] = total.astype(BF16)
    for d in range(1, highs):
        send(planes.at[member], planes.at[member], s3.at[d - 1], r3.at[d - 1],
             facet=group + lax.rem(member + d, highs))
    for d in range(1, highs):
        there = lax.rem(member + highs - d, highs)
        remote(planes.at[there], planes.at[there], s3.at[d - 1], r3.at[d - 1],
               facet=beside).wait_recv()
    y = nn(kernel[...], flat(planes[...])).astype(BF16)
    z = nt(y, kernel[...])
    w = (weight * z).astype(BF16)
    u = nn(w, kernel[...]).astype(BF16)
    first_row = pl.multiple_of(member * piece, piece)
    result = nn(kernel_t[pl.ds(first_row, piece), :], u)
    grids[sub_at, band_at, facet_at] = result.astype(BF16)

    def origin(e):
        return lax.rem(band_at + band_count - e, band_count)

    def to_core(b, f):
        ref = grids.at[sub_at, b, f]
        for d in range(1, sub_count):
            send(ref, ref, s6.at[d - 1, b, f], r6.at[d - 1, b, f],
                 sub=lax.rem(sub_at + d, sub_count))

    def to_beside(b, f):
        ref = grids.at[sub_at, b, f]
        send(ref, ref, slo.at[b, f], r5.at[b, f], facet=beside)

    def to_highs(b, f, slot):
        ref = grids.at[sub_at, b, f]
        for d in range(1, highs):
            send(ref, ref, shi.at[slot, b, d - 1], r5.at[b, f], facet=2 * across(d) + low)

    def arrived(b, f):
        ref = grids.at[sub_at, b, f]
        remote(ref, ref, slo.at[b, f], r5.at[b, f], facet=beside).wait_recv()

    def fan(e):
        b = origin(e)
        if e > 0:
            ref = grids.at[sub_at, b, facet_at]
            remote(ref, ref, s4.at[e - 1], r4.at[e - 1], band=b).wait_recv()
        to_beside(b, facet_at)
        to_highs(b, facet_at, 0)
        to_core(b, facet_at)

    def forward(e):
        b = origin(e)
        arrived(b, beside)
        if e % 2 == 0:
            to_highs(b, beside, 1)
        to_core(b, beside)
        for d in range(1, highs):
            f = 2 * across(d) + low
            arrived(b, f)
            if e % 2 == 1:
                to_beside(b, f)
            to_core(b, f)

    def finish(e):
        b = origin(e)
        for d in range(1, highs):
            f = 2 * across(d) + 1 - low
            arrived(b, f)
            to_core(b, f)

    for d in range(1, band_count):
        ref = grids.at[sub_at, band_at, facet_at]
        send(ref, ref, s4.at[d - 1], r4.at[d - 1], band=lax.rem(band_at + d, band_count))

    def gather(sub, b, fresh):
        s = sub * band_count + b
        block = flat(grids[sub, b])
        if fresh:
            by_cos[...] = nt(cos_tab[s], block)
            by_sin[...] = nt(sin_tab[s], block)
        else:
            by_cos[...] += nt(cos_tab[s], block)
            by_sin[...] += nt(sin_tab[s], block)

    def gather_other(e):
        b = origin(e)
        for d in range(1, sub_count):
            other = lax.rem(sub_at + d, sub_count)
            for f in range(facet_count):
                ref = grids.at[other, b, f]
                remote(ref, ref, s6.at[d - 1, b, f], r6.at[d - 1, b, f], sub=other).wait_recv()
            gather(other, b, False)

    order = [d for pair in zip(range(1, band_count), range(band_count - 1, 0, -1)) for d in pair]
    order = [0] + list(dict.fromkeys(order))
    fan(order[0])
    column_tables(column[0], offset_y, contrib, width, store_plain)
    table = pltpu.make_async_copy(out_cols, table_hbm, table_sem)
    table.start()
    for before, e in zip(order, order[1:]):
        fan(e)
        forward(before)
    forward(order[-1])
    finish(order[0])
    gather(sub_at, origin(order[0]), True)
    for before, e in zip(order, order[1:]):
        finish(e)
        gather_other(before)
        gather(sub_at, origin(e), False)
    gather_other(order[-1])
    real = (by_cos[:, :contrib] - by_sin[:, contrib:]) * back_scale
    imag = (by_cos[:, contrib:] + by_sin[:, :contrib]) * back_scale
    out[:, :contrib] = real.astype(BF16)
    out[:, contrib:] = (-imag).astype(BF16)
    table.wait()
    for copy in started:
        copy.wait_send()


def image_kernel(both, table, taper, out):
    scale = 1.0 / math.sqrt(both.shape[1] // 2)
    out[...] = (taper[...] * scale * nn(both[...], table[...])).astype(BF16)


def body(sizes, facets, window, facet_offsets, row_offsets, column_offset, kernel, tile_counts):
    facet_count, band_count, sub_count = sizes
    rows, width = facets.shape
    contrib = kernel.shape[0]
    subgrids = row_offsets.shape[0]
    piece = 2 * contrib // facet_count
    highs = facet_count // 2
    more = max(highs - 1, 1)
    smem = pl.BlockSpec(memory_space=pltpu.SMEM)
    vmem = pl.BlockSpec(memory_space=pltpu.VMEM)
    anywhere = pl.BlockSpec(memory_space=pl.ANY)
    taper = window.reshape(1, width)
    dma = pltpu.SemaphoreType.DMA

    def buffer(*shape, dtype=BF16):
        return pltpu.VMEM(shape, dtype)

    both, table = pl.pallas_call(
        exchange_kernel,
        out_shape=(
            jax.ShapeDtypeStruct((rows, 2 * contrib), BF16),
            jax.ShapeDtypeStruct((2 * contrib, width), BF16),
        ),
        in_specs=[smem, smem, smem, anywhere, vmem, vmem, vmem],
        out_specs=(vmem, anywhere),
        scratch_shapes=[
            buffer(rows, width),
            buffer(2 * contrib, width),
            buffer(2 * contrib, 2 * rows),
            buffer(subgrids, rows, contrib),
            buffer(subgrids, rows, contrib),
            buffer(2 * contrib, width),
            buffer(contrib, contrib),
            buffer(band_count, facet_count, piece, contrib),
            buffer(band_count, highs, piece, contrib),
            buffer(band_count, more, piece, contrib),
            buffer(band_count, more, 2, piece, contrib),
            buffer(band_count, piece, contrib),
            buffer(band_count, more, piece, contrib),
            buffer(band_count, piece, contrib),
            buffer(band_count - 1, piece, contrib),
            buffer(band_count - 1, piece, contrib),
            buffer(highs, piece, contrib),
            buffer(sub_count, band_count, facet_count, piece, contrib),
            buffer(rows, 2 * contrib, dtype=F32),
            buffer(rows, 2 * contrib, dtype=F32),
            dma,
            dma,
        ]
        + [dma((band_count, highs))] * 2
        + [dma((band_count, more))] * 4
        + [dma((band_count,))] * 2
        + [dma((band_count - 1,))] * 2
        + [dma((more,))] * 2
        + [dma((band_count - 1,))] * 2
        + [
            dma((band_count, facet_count)),
            dma((2, band_count, more)),
            dma((band_count, facet_count)),
        ]
        + [dma((max(sub_count - 1, 1), band_count, facet_count))] * 2,
        compiler_params=pltpu.CompilerParams(collective_id=0, has_side_effects=True),
        name="exchange",
    )(facet_offsets.T, row_offsets, column_offset, facets, taper, kernel, tile_counts)
    wide = min(width, 512)
    return pl.pallas_call(
        image_kernel,
        grid=(width // wide,),
        out_shape=jax.ShapeDtypeStruct((rows, width), BF16),
        in_specs=[
            pl.BlockSpec((rows, 2 * contrib), lambda i: (0, 0)),
            pl.BlockSpec((2 * contrib, wide), lambda i: (0, i)),
            pl.BlockSpec((1, wide), lambda i: (0, i)),
        ],
        out_specs=pl.BlockSpec((rows, wide), lambda i: (0, i)),
        name="image",
    )(both, table, taper)


def solution(mesh):
    sizes = tuple(mesh.shape[axis] for axis in ("facet", "band", "sub"))
    in_specs = (P(("facet", "band"), None), P(), P(), P(), P(), P(), P())
    out_specs = P(("facet", "band"), None)
    return jax.shard_map(
        functools.partial(body, sizes), mesh=mesh, in_specs=in_specs, out_specs=out_specs, check_vma=False
    )
```

```python
import functools
import math

import jax
import jax.numpy as jnp
from jax import lax
from jax.experimental import pallas as pl
from jax.experimental.pallas import tpu as pltpu
from jax.sharding import PartitionSpec as P

IMAGE = 49152
QUARTER = IMAGE // 4
LANES = 128
FINE = 32
F32 = jnp.float32
BF16 = jnp.bfloat16
I32 = jnp.int32


def wrap(value):
    return value - float(IMAGE) * jnp.floor(value * (1.0 / IMAGE))


def phase_pair(first, second):
    upper = (first >> 8).astype(F32)
    lower = (first & 255).astype(F32)
    other = second.astype(F32)
    reduced = wrap(wrap(upper * other) * 256.0)
    reduced = wrap(reduced + lower * other)
    turn = jnp.floor(reduced * (1.0 / QUARTER) + 0.5)
    angle = (reduced - turn * float(QUARTER)) * (2.0 * math.pi / IMAGE)
    square = angle * angle
    sine = 1.0 / 120 + square * (-1.0 / 5040 + square * (1.0 / 362880))
    sine = angle + angle * square * (-1.0 / 6 + square * sine)
    cosine = -1.0 / 720 + square * (1.0 / 40320 + square * (-1.0 / 3628800))
    cosine = 1.0 + square * (-0.5 + square * (1.0 / 24 + square * cosine))
    quadrant = turn.astype(I32)
    odd = (quadrant & 1) == 1
    real = jnp.where(odd, sine, cosine)
    imag = jnp.where(odd, cosine, sine)
    real = jnp.where(((quadrant + 1) & 2) != 0, -real, real)
    imag = jnp.where((quadrant & 2) != 0, -imag, imag)
    return real, imag


def iota(shape, dim):
    return lax.broadcasted_iota(I32, shape, dim)


def nt(left, right):
    return lax.dot_general(left, right, (((1,), (1,)), ((), ())), preferred_element_type=F32)


def nn(left, right):
    return jnp.dot(left, right, preferred_element_type=F32)


def column_tables(column, offset, contrib, width, store):
    shape = (contrib, LANES)
    freq = column + iota(shape, 0)
    lane = iota(shape, 1)
    coarse_c, coarse_s = phase_pair(freq, offset + LANES * lane)
    fine_c, fine_s = phase_pair(freq, lane)
    for at in range(width // LANES):
        c = coarse_c[:, at : at + 1]
        s = coarse_s[:, at : at + 1]
        store(at, c * fine_c - s * fine_s, s * fine_c + c * fine_s)


def row_tables(start, offset, rows, contrib, store):
    coarse = rows // FINE
    cc, cs = phase_pair(
        start + iota((coarse, contrib), 1), offset + FINE * iota((coarse, contrib), 0)
    )
    fc, fs = phase_pair(start + iota((FINE, contrib), 1), iota((FINE, contrib), 0))
    for at in range(coarse):
        c = cc[at : at + 1, :]
        s = cs[at : at + 1, :]
        store(at * FINE, (c * fc - s * fs).astype(BF16), (s * fc + c * fs).astype(BF16))


def flat(block):
    pieces, rows, contrib = block.shape
    if rows % 16:
        return block.astype(F32).reshape(pieces * rows, contrib).astype(BF16)
    return block.reshape(pieces * rows, contrib)


def exchange_kernel(
    offsets, starts, column, facets_hbm, taper, kernel, counts,
    out, out_cols,
    facets, cols, left, cos_tab, sin_tab, kernel_t, parts,
    recv_a, recv_b, recv_c, recv_d, mid_a, mid_d, own2, recv2, planes, grids, by_cos, by_sin,
    load_sem,
    sa, ra, sb, rb, sc, rc, sd, rd, s2, r2, s3, r3, s4, r4, slo, shi, r5, s6, r6,
):
    facet_at = lax.axis_index("facet")
    band_at = lax.axis_index("band")
    sub_at = lax.axis_index("sub")
    band_count, facet_count, piece, contrib = parts.shape
    sub_count = grids.shape[0]
    rows, width = facets.shape
    highs = facet_count // 2
    high = facet_at // 2
    low = facet_at % 2
    beside = high * 2 + (1 - low)
    group = (facet_at // highs) * highs
    member = facet_at % highs
    b_scale = 1.0 / math.sqrt(width)
    a_scale = 1.0 / math.sqrt(width * facet_count)
    back_scale = 1.0 / math.sqrt(sub_count * band_count * contrib)
    started = []

    def remote(src, dst, send, recv, **where):
        return pltpu.make_async_remote_copy(
            src_ref=src, dst_ref=dst, send_sem=send, recv_sem=recv,
            device_id=where, device_id_type=pl.DeviceIdType.MESH,
        )

    def send(*args, **where):
        copy = remote(*args, **where)
        copy.start()
        started.append(copy)

    def across(d):
        return lax.rem(high + d, highs)

    load = pltpu.make_async_copy(facets_hbm, facets, load_sem)
    load.start()
    barrier = pltpu.get_barrier_semaphore()
    for axis, at, count in (
        ("facet", facet_at, facet_count), ("band", band_at, band_count), ("sub", sub_at, sub_count)
    ):
        for d in range(1, count):
            pl.semaphore_signal(barrier, 1, device_id={axis: lax.rem(at + d, count)},
                                device_id_type=pl.DeviceIdType.MESH)

    def store_taper(at, cosine, sine):
        here = slice(at * LANES, (at + 1) * LANES)
        cols[0:contrib, here] = (cosine * taper[:, here]).astype(BF16)
        cols[contrib:, here] = (sine * taper[:, here]).astype(BF16)

    def store_plain(at, cosine, sine):
        here = slice(at * LANES, (at + 1) * LANES)
        out_cols[0:contrib, here] = cosine.astype(BF16)
        out_cols[contrib:, here] = sine.astype(BF16)

    offset_y = offsets[1, facet_at]
    position = offsets[0, facet_at] + band_at * rows

    def make_rows(s):
        def store_row(at, cosine, sine):
            cos_tab[s, at : at + FINE, :] = cosine
            sin_tab[s, at : at + FINE, :] = sine

        row_tables(starts[s], position, rows, contrib, store_row)

    column_tables(column[0], offset_y, contrib, width, store_taper)
    load.wait()
    t = nt(cols[...], facets[...]) * b_scale
    t_real = t[:contrib].astype(BF16)
    t_imag = (-t[contrib:]).astype(BF16)
    left[:contrib, :rows] = t_real
    left[:contrib, rows:] = t_imag
    left[contrib:, :rows] = t_imag
    left[contrib:, rows:] = -t_real

    def owner(e):
        return lax.rem(band_at + 1 + e, band_count)

    for e in range(band_count):
        g = owner(e)
        s = sub_at * band_count + g
        make_rows(s)
        part = (nn(left[:, :rows], cos_tab[s]) + nn(left[:, rows:], sin_tab[s])) * a_scale
        for f in range(facet_count):
            parts[g, f] = part[f * piece : (f + 1) * piece].astype(BF16)
        if e == 0:
            pl.semaphore_wait(barrier, facet_count + band_count + sub_count - 3)
        if e % 2 == 0:
            for h in range(highs):
                send(parts.at[g, 2 * h + 1 - low], recv_a.at[e, h], sa.at[e, h], ra.at[e, h],
                     facet=beside)
        else:
            for d in range(1, highs):
                send(parts.at[g, pl.ds(2 * across(d), 2)], recv_c.at[e, d - 1], sc.at[e, d - 1],
                     rc.at[e, d - 1], facet=2 * across(d) + low)
    for d in range(1, sub_count):
        def other_rows(b, carry, d=d):
            make_rows(lax.rem(sub_at + d, sub_count) * band_count + b)
            return carry

        lax.fori_loop(0, band_count, other_rows, 0)

    def second_hop(e):
        g = owner(e)
        if e % 2 == 0:
            for h in range(highs):
                remote(parts.at[g, 0], recv_a.at[e, h], sa.at[e, h], ra.at[e, h],
                       facet=beside).wait_recv()
            for d in range(1, highs):
                h = across(d)
                mine = parts[g, 2 * h + low].astype(F32) + recv_a[e, h].astype(F32)
                mid_a[e, d - 1] = mine.astype(BF16)
                send(mid_a.at[e, d - 1], recv_b.at[e, d - 1], sb.at[e, d - 1], rb.at[e, d - 1],
                     facet=2 * h + low)
        else:
            mine = parts[g, beside].astype(F32)
            for d in range(1, highs):
                remote(parts.at[g, pl.ds(0, 2)], recv_c.at[e, d - 1], sc.at[e, d - 1],
                       rc.at[e, d - 1], facet=beside).wait_recv()
                mine = mine + recv_c[e, d - 1, 1 - low].astype(F32)
            mid_d[e] = mine.astype(BF16)
            send(mid_d.at[e], recv_d.at[e], sd.at[e], rd.at[e], facet=beside)

    def facet_sum(e):
        g = owner(e)
        total = parts[g, facet_at].astype(F32)
        if e % 2 == 0:
            total = total + recv_a[e, high].astype(F32)
            for d in range(1, highs):
                remote(mid_a.at[e, d - 1], recv_b.at[e, d - 1], sb.at[e, d - 1], rb.at[e, d - 1],
                       facet=beside).wait_recv()
                total = total + recv_b[e, d - 1].astype(F32)
        else:
            for d in range(1, highs):
                total = total + recv_c[e, d - 1, low].astype(F32)
            remote(mid_d.at[e], recv_d.at[e], sd.at[e], rd.at[e], facet=beside).wait_recv()
            total = total + recv_d[e].astype(F32)
        if e < band_count - 1:
            own2[e] = total.astype(BF16)
            send(own2.at[e], recv2.at[e], s2.at[e], r2.at[e], band=g)
        return total

    second_hop(0)
    for e in range(1, band_count):
        second_hop(e)
        facet_sum(e - 1)
    kernel_t[...] = kernel[...].T
    tiles = counts.shape[1]
    side = contrib // tiles
    spread = (iota((contrib, tiles), 0) // side == iota((contrib, tiles), 1)).astype(BF16)
    tile = counts[sub_at * band_count + band_at].astype(F32).astype(BF16)
    seen = nt(nt(spread, tile).astype(BF16), spread)
    weight = seen / (seen + 4.0)
    total = facet_sum(band_count - 1)
    for e in range(band_count - 1):
        remote(own2.at[e], recv2.at[e], s2.at[e], r2.at[e], band=band_at).wait_recv()
        total = total + recv2[e].astype(F32)
    planes[member] = total.astype(BF16)
    for d in range(1, highs):
        send(planes.at[member], planes.at[member], s3.at[d - 1], r3.at[d - 1],
             facet=group + lax.rem(member + d, highs))
    for d in range(1, highs):
        there = lax.rem(member + highs - d, highs)
        remote(planes.at[there], planes.at[there], s3.at[d - 1], r3.at[d - 1],
               facet=beside).wait_recv()
    y = nn(kernel[...], flat(planes[...])).astype(BF16)
    z = nt(y, kernel[...])
    w = (weight * z).astype(BF16)
    u = nn(w, kernel[...]).astype(BF16)
    first_row = pl.multiple_of(member * piece, piece)
    result = nn(kernel_t[pl.ds(first_row, piece), :], u)
    grids[sub_at, band_at, facet_at] = result.astype(BF16)

    def origin(e):
        return lax.rem(band_at + band_count - e, band_count)

    def to_core(b, f):
        ref = grids.at[sub_at, b, f]
        for d in range(1, sub_count):
            send(ref, ref, s6.at[d - 1, b, f], r6.at[d - 1, b, f],
                 sub=lax.rem(sub_at + d, sub_count))

    def to_beside(b, f):
        ref = grids.at[sub_at, b, f]
        send(ref, ref, slo.at[b, f], r5.at[b, f], facet=beside)

    def to_highs(b, f, slot):
        ref = grids.at[sub_at, b, f]
        for d in range(1, highs):
            send(ref, ref, shi.at[slot, b, d - 1], r5.at[b, f], facet=2 * across(d) + low)

    def arrived(b, f):
        ref = grids.at[sub_at, b, f]
        remote(ref, ref, slo.at[b, f], r5.at[b, f], facet=beside).wait_recv()

    def fan(e):
        b = origin(e)
        if e > 0:
            ref = grids.at[sub_at, b, facet_at]
            remote(ref, ref, s4.at[e - 1], r4.at[e - 1], band=b).wait_recv()
        to_beside(b, facet_at)
        to_highs(b, facet_at, 0)
        to_core(b, facet_at)

    def forward(e):
        b = origin(e)
        arrived(b, beside)
        if e % 2 == 0:
            to_highs(b, beside, 1)
        to_core(b, beside)
        for d in range(1, highs):
            f = 2 * across(d) + low
            arrived(b, f)
            if e % 2 == 1:
                to_beside(b, f)
            to_core(b, f)

    def finish(e):
        b = origin(e)
        for d in range(1, highs):
            f = 2 * across(d) + 1 - low
            arrived(b, f)
            to_core(b, f)

    for d in range(1, band_count):
        ref = grids.at[sub_at, band_at, facet_at]
        send(ref, ref, s4.at[d - 1], r4.at[d - 1], band=lax.rem(band_at + d, band_count))

    def gather(sub, b, fresh):
        s = sub * band_count + b
        block = flat(grids[sub, b])
        if fresh:
            by_cos[...] = nt(cos_tab[s], block)
            by_sin[...] = nt(sin_tab[s], block)
        else:
            by_cos[...] += nt(cos_tab[s], block)
            by_sin[...] += nt(sin_tab[s], block)

    def gather_other(e):
        b = origin(e)
        for d in range(1, sub_count):
            other = lax.rem(sub_at + d, sub_count)
            for f in range(facet_count):
                ref = grids.at[other, b, f]
                remote(ref, ref, s6.at[d - 1, b, f], r6.at[d - 1, b, f], sub=other).wait_recv()
            gather(other, b, False)

    order = [d for pair in zip(range(1, band_count), range(band_count - 1, 0, -1)) for d in pair]
    order = [0] + list(dict.fromkeys(order))
    fan(order[0])
    column_tables(column[0], offset_y, contrib, width, store_plain)
    for before, e in zip(order, order[1:]):
        fan(e)
        forward(before)
    forward(order[-1])
    finish(order[0])
    gather(sub_at, origin(order[0]), True)
    for before, e in zip(order, order[1:]):
        finish(e)
        gather_other(before)
        gather(sub_at, origin(e), False)
    gather_other(order[-1])
    real = (by_cos[:, :contrib] - by_sin[:, contrib:]) * back_scale
    imag = (by_cos[:, contrib:] + by_sin[:, :contrib]) * back_scale
    out[:, :contrib] = real.astype(BF16)
    out[:, contrib:] = (-imag).astype(BF16)
    for copy in started:
        copy.wait_send()


def image_kernel(both, table, taper, out):
    scale = 1.0 / math.sqrt(both.shape[1] // 2)
    wide = out.shape[1]
    here = pl.ds(pl.multiple_of(pl.program_id(0) * wide, wide), wide)
    out[...] = (taper[:, here] * scale * nn(both[...], table[:, here])).astype(BF16)


def body(sizes, facets, window, facet_offsets, row_offsets, column_offset, kernel, tile_counts):
    facet_count, band_count, sub_count = sizes
    rows, width = facets.shape
    contrib = kernel.shape[0]
    subgrids = row_offsets.shape[0]
    piece = 2 * contrib // facet_count
    highs = facet_count // 2
    more = max(highs - 1, 1)
    smem = pl.BlockSpec(memory_space=pltpu.SMEM)
    vmem = pl.BlockSpec(memory_space=pltpu.VMEM)
    anywhere = pl.BlockSpec(memory_space=pl.ANY)
    taper = window.reshape(1, width)
    dma = pltpu.SemaphoreType.DMA

    def buffer(*shape, dtype=BF16):
        return pltpu.VMEM(shape, dtype)

    both, table = pl.pallas_call(
        exchange_kernel,
        out_shape=(
            pltpu.VMEM((rows, 2 * contrib), BF16),
            pltpu.VMEM((2 * contrib, width), BF16),
        ),
        in_specs=[smem, smem, smem, anywhere, vmem, vmem, vmem],
        out_specs=(vmem, vmem),
        scratch_shapes=[
            buffer(rows, width),
            buffer(2 * contrib, width),
            buffer(2 * contrib, 2 * rows),
            buffer(subgrids, rows, contrib),
            buffer(subgrids, rows, contrib),
            buffer(contrib, contrib),
            buffer(band_count, facet_count, piece, contrib),
            buffer(band_count, highs, piece, contrib),
            buffer(band_count, more, piece, contrib),
            buffer(band_count, more, 2, piece, contrib),
            buffer(band_count, piece, contrib),
            buffer(band_count, more, piece, contrib),
            buffer(band_count, piece, contrib),
            buffer(band_count - 1, piece, contrib),
            buffer(band_count - 1, piece, contrib),
            buffer(highs, piece, contrib),
            buffer(sub_count, band_count, facet_count, piece, contrib),
            buffer(rows, 2 * contrib, dtype=F32),
            buffer(rows, 2 * contrib, dtype=F32),
            dma,
        ]
        + [dma((band_count, highs))] * 2
        + [dma((band_count, more))] * 4
        + [dma((band_count,))] * 2
        + [dma((band_count - 1,))] * 2
        + [dma((more,))] * 2
        + [dma((band_count - 1,))] * 2
        + [
            dma((band_count, facet_count)),
            dma((2, band_count, more)),
            dma((band_count, facet_count)),
        ]
        + [dma((max(sub_count - 1, 1), band_count, facet_count))] * 2,
        compiler_params=pltpu.CompilerParams(
            collective_id=0, has_side_effects=True
        ),
        name="exchange",
    )(facet_offsets.T, row_offsets, column_offset, facets, taper, kernel, tile_counts)
    wide = min(width, 512)
    both = pltpu.with_memory_space_constraint(both, pltpu.VMEM)
    table = pltpu.with_memory_space_constraint(table, pltpu.VMEM)
    return pl.pallas_call(
        image_kernel,
        grid=(width // wide,),
        out_shape=jax.ShapeDtypeStruct((rows, width), BF16),
        in_specs=[vmem, vmem, vmem],
        out_specs=pl.BlockSpec((rows, wide), lambda i: (0, i)),
        compiler_params=pltpu.CompilerParams(vmem_limit_bytes=16 << 20),
        name="image",
    )(both, table, taper)


def solution(mesh):
    sizes = tuple(mesh.shape[axis] for axis in ("facet", "band", "sub"))
    in_specs = (P(("facet", "band"), None), P(), P(), P(), P(), P(), P())
    out_specs = P(("facet", "band"), None)
    return jax.shard_map(
        functools.partial(body, sizes), mesh=mesh, in_specs=in_specs, out_specs=out_specs, check_vma=False
    )
```

```python
import functools
import math

import jax
import jax.numpy as jnp
from jax import lax
from jax.experimental import pallas as pl
from jax.experimental.pallas import tpu as pltpu
from jax.sharding import PartitionSpec as P

IMAGE = 49152
QUARTER = IMAGE // 4
LANES = 128
FINE = 32
F32 = jnp.float32
BF16 = jnp.bfloat16
I32 = jnp.int32


def wrap(value):
    return value - float(IMAGE) * jnp.floor(value * (1.0 / IMAGE))


def phase_pair(first, second):
    upper = (first >> 8).astype(F32)
    lower = (first & 255).astype(F32)
    other = second.astype(F32)
    reduced = wrap(wrap(upper * other) * 256.0)
    reduced = wrap(reduced + lower * other)
    turn = jnp.floor(reduced * (1.0 / QUARTER) + 0.5)
    angle = (reduced - turn * float(QUARTER)) * (2.0 * math.pi / IMAGE)
    square = angle * angle
    sine = 1.0 / 120 + square * (-1.0 / 5040 + square * (1.0 / 362880))
    sine = angle + angle * square * (-1.0 / 6 + square * sine)
    cosine = -1.0 / 720 + square * (1.0 / 40320 + square * (-1.0 / 3628800))
    cosine = 1.0 + square * (-0.5 + square * (1.0 / 24 + square * cosine))
    quadrant = turn.astype(I32)
    odd = (quadrant & 1) == 1
    real = jnp.where(odd, sine, cosine)
    imag = jnp.where(odd, cosine, sine)
    real = jnp.where(((quadrant + 1) & 2) != 0, -real, real)
    imag = jnp.where((quadrant & 2) != 0, -imag, imag)
    return real, imag


def iota(shape, dim):
    return lax.broadcasted_iota(I32, shape, dim)


def nt(left, right):
    return lax.dot_general(left, right, (((1,), (1,)), ((), ())), preferred_element_type=F32)


def nn(left, right):
    return jnp.dot(left, right, preferred_element_type=F32)


def column_tables(column, offset, contrib, width, store):
    shape = (contrib, LANES)
    freq = column + iota(shape, 0)
    lane = iota(shape, 1)
    coarse_c, coarse_s = phase_pair(freq, offset + LANES * lane)
    fine_c, fine_s = phase_pair(freq, lane)
    for at in range(width // LANES):
        c = coarse_c[:, at : at + 1]
        s = coarse_s[:, at : at + 1]
        store(at, c * fine_c - s * fine_s, s * fine_c + c * fine_s)


def row_tables(start, offset, rows, contrib, store):
    coarse = rows // FINE
    cc, cs = phase_pair(
        start + iota((coarse, contrib), 1), offset + FINE * iota((coarse, contrib), 0)
    )
    fc, fs = phase_pair(start + iota((FINE, contrib), 1), iota((FINE, contrib), 0))
    for at in range(coarse):
        c = cc[at : at + 1, :]
        s = cs[at : at + 1, :]
        store(at * FINE, (c * fc - s * fs).astype(BF16), (s * fc + c * fs).astype(BF16))


def flat(block):
    pieces, rows, contrib = block.shape
    if rows % 16:
        return block.astype(F32).reshape(pieces * rows, contrib).astype(BF16)
    return block.reshape(pieces * rows, contrib)


def exchange_kernel(
    offsets, starts, column, facets_hbm, taper, kernel, counts,
    out, out_cols,
    facets, cols, left, cos_tab, sin_tab, kernel_t, parts,
    recv_a, recv_b, recv_c, recv_d, mid_a, mid_d, own2, recv2, planes, grids, by_cos, by_sin,
    load_sem,
    sa, ra, sb, rb, sc, rc, sd, rd, s2, r2, s3, r3, s4, r4, slo, shi, r5, s6, r6,
):
    facet_at = lax.axis_index("facet")
    band_at = lax.axis_index("band")
    sub_at = lax.axis_index("sub")
    band_count, facet_count, piece, contrib = parts.shape
    sub_count = grids.shape[0]
    rows, width = facets.shape
    highs = facet_count // 2
    high = facet_at // 2
    low = facet_at % 2
    beside = high * 2 + (1 - low)
    group = (facet_at // highs) * highs
    member = facet_at % highs
    b_scale = 1.0 / math.sqrt(width)
    a_scale = 1.0 / math.sqrt(width * facet_count)
    back_scale = 1.0 / math.sqrt(sub_count * band_count * contrib)
    started = []

    def remote(src, dst, send, recv, **where):
        return pltpu.make_async_remote_copy(
            src_ref=src, dst_ref=dst, send_sem=send, recv_sem=recv,
            device_id=where, device_id_type=pl.DeviceIdType.MESH,
        )

    def send(*args, **where):
        copy = remote(*args, **where)
        copy.start()
        started.append(copy)

    def across(d):
        return lax.rem(high + d, highs)

    load = pltpu.make_async_copy(facets_hbm, facets, load_sem)
    load.start()
    barrier = pltpu.get_barrier_semaphore()
    for axis, at, count in (
        ("facet", facet_at, facet_count), ("band", band_at, band_count), ("sub", sub_at, sub_count)
    ):
        for d in range(1, count):
            pl.semaphore_signal(barrier, 1, device_id={axis: lax.rem(at + d, count)},
                                device_id_type=pl.DeviceIdType.MESH)

    def store_taper(at, cosine, sine):
        here = slice(at * LANES, (at + 1) * LANES)
        cols[0:contrib, here] = (cosine * taper[:, here]).astype(BF16)
        cols[contrib:, here] = (sine * taper[:, here]).astype(BF16)

    def store_plain(at, cosine, sine):
        here = slice(at * LANES, (at + 1) * LANES)
        out_cols[0:contrib, here] = cosine.astype(BF16)
        out_cols[contrib:, here] = sine.astype(BF16)

    offset_y = offsets[1, facet_at]
    position = offsets[0, facet_at] + band_at * rows

    def make_rows(s):
        def store_row(at, cosine, sine):
            cos_tab[s, at : at + FINE, :] = cosine
            sin_tab[s, at : at + FINE, :] = sine

        row_tables(starts[s], position, rows, contrib, store_row)

    column_tables(column[0], offset_y, contrib, width, store_taper)
    load.wait()
    t = nt(cols[...], facets[...]) * b_scale
    t_real = t[:contrib].astype(BF16)
    t_imag = (-t[contrib:]).astype(BF16)
    left[:contrib, :rows] = t_real
    left[:contrib, rows:] = t_imag
    left[contrib:, :rows] = t_imag
    left[contrib:, rows:] = -t_real

    shifts = sorted(range(1, band_count), key=lambda d: abs(2 * d - band_count)) + [0]

    def owner(e):
        return lax.rem(band_at + shifts[e], band_count)

    for e in range(band_count):
        g = owner(e)
        s = sub_at * band_count + g
        make_rows(s)
        part = (nn(left[:, :rows], cos_tab[s]) + nn(left[:, rows:], sin_tab[s])) * a_scale
        for f in range(facet_count):
            parts[g, f] = part[f * piece : (f + 1) * piece].astype(BF16)
        if e == 0:
            pl.semaphore_wait(barrier, facet_count + band_count + sub_count - 3)
        if e % 2 == 0:
            for h in range(highs):
                send(parts.at[g, 2 * h + 1 - low], recv_a.at[e, h], sa.at[e, h], ra.at[e, h],
                     facet=beside)
        else:
            for d in range(1, highs):
                send(parts.at[g, pl.ds(2 * across(d), 2)], recv_c.at[e, d - 1], sc.at[e, d - 1],
                     rc.at[e, d - 1], facet=2 * across(d) + low)
    for d in range(1, sub_count):
        def other_rows(b, carry, d=d):
            make_rows(lax.rem(sub_at + d, sub_count) * band_count + b)
            return carry

        lax.fori_loop(0, band_count, other_rows, 0)
    column_tables(column[0], offset_y, contrib, width, store_plain)

    def second_hop(e):
        g = owner(e)
        if e % 2 == 0:
            for h in range(highs):
                remote(parts.at[g, 0], recv_a.at[e, h], sa.at[e, h], ra.at[e, h],
                       facet=beside).wait_recv()
            for d in range(1, highs):
                h = across(d)
                mine = parts[g, 2 * h + low].astype(F32) + recv_a[e, h].astype(F32)
                mid_a[e, d - 1] = mine.astype(BF16)
                send(mid_a.at[e, d - 1], recv_b.at[e, d - 1], sb.at[e, d - 1], rb.at[e, d - 1],
                     facet=2 * h + low)
        else:
            mine = parts[g, beside].astype(F32)
            for d in range(1, highs):
                remote(parts.at[g, pl.ds(0, 2)], recv_c.at[e, d - 1], sc.at[e, d - 1],
                       rc.at[e, d - 1], facet=beside).wait_recv()
                mine = mine + recv_c[e, d - 1, 1 - low].astype(F32)
            mid_d[e] = mine.astype(BF16)
            send(mid_d.at[e], recv_d.at[e], sd.at[e], rd.at[e], facet=beside)

    def facet_sum(e):
        g = owner(e)
        total = parts[g, facet_at].astype(F32)
        if e % 2 == 0:
            total = total + recv_a[e, high].astype(F32)
            for d in range(1, highs):
                remote(mid_a.at[e, d - 1], recv_b.at[e, d - 1], sb.at[e, d - 1], rb.at[e, d - 1],
                       facet=beside).wait_recv()
                total = total + recv_b[e, d - 1].astype(F32)
        else:
            for d in range(1, highs):
                total = total + recv_c[e, d - 1, low].astype(F32)
            remote(mid_d.at[e], recv_d.at[e], sd.at[e], rd.at[e], facet=beside).wait_recv()
            total = total + recv_d[e].astype(F32)
        if e < band_count - 1:
            own2[e] = total.astype(BF16)
            send(own2.at[e], recv2.at[e], s2.at[e], r2.at[e], band=g)
        return total

    second_hop(0)
    for e in range(1, band_count):
        second_hop(e)
        facet_sum(e - 1)
    kernel_t[...] = kernel[...].T
    tiles = counts.shape[1]
    side = contrib // tiles
    spread = (iota((contrib, tiles), 0) // side == iota((contrib, tiles), 1)).astype(BF16)
    tile = counts[sub_at * band_count + band_at].astype(F32).astype(BF16)
    seen = nt(nt(spread, tile).astype(BF16), spread)
    weight = seen / (seen + 4.0)
    total = facet_sum(band_count - 1)
    for e in range(band_count - 1):
        remote(own2.at[e], recv2.at[e], s2.at[e], r2.at[e], band=band_at).wait_recv()
        total = total + recv2[e].astype(F32)
    planes[member] = total.astype(BF16)
    for d in range(1, highs):
        send(planes.at[member], planes.at[member], s3.at[d - 1], r3.at[d - 1],
             facet=group + lax.rem(member + d, highs))
    for d in range(1, highs):
        there = lax.rem(member + highs - d, highs)
        remote(planes.at[there], planes.at[there], s3.at[d - 1], r3.at[d - 1],
               facet=beside).wait_recv()
    y = nn(kernel[...], flat(planes[...])).astype(BF16)
    z = nt(y, kernel[...])
    w = (weight * z).astype(BF16)
    u = nn(w, kernel[...]).astype(BF16)
    first_row = pl.multiple_of(member * piece, piece)
    result = nn(kernel_t[pl.ds(first_row, piece), :], u)
    grids[sub_at, band_at, facet_at] = result.astype(BF16)

    def origin(e):
        return lax.rem(band_at + band_count - e, band_count)

    def to_core(b, f):
        ref = grids.at[sub_at, b, f]
        for d in range(1, sub_count):
            send(ref, ref, s6.at[d - 1, b, f], r6.at[d - 1, b, f],
                 sub=lax.rem(sub_at + d, sub_count))

    def to_beside(b, f):
        ref = grids.at[sub_at, b, f]
        send(ref, ref, slo.at[b, f], r5.at[b, f], facet=beside)

    def to_highs(b, f, slot):
        ref = grids.at[sub_at, b, f]
        for d in range(1, highs):
            send(ref, ref, shi.at[slot, b, d - 1], r5.at[b, f], facet=2 * across(d) + low)

    def arrived(b, f):
        ref = grids.at[sub_at, b, f]
        remote(ref, ref, slo.at[b, f], r5.at[b, f], facet=beside).wait_recv()

    def fan(e):
        b = origin(e)
        if e > 0:
            ref = grids.at[sub_at, b, facet_at]
            remote(ref, ref, s4.at[e - 1], r4.at[e - 1], band=b).wait_recv()
        to_beside(b, facet_at)
        to_highs(b, facet_at, 0)
        to_core(b, facet_at)

    def forward(e):
        b = origin(e)
        arrived(b, beside)
        if e % 2 == 0:
            to_highs(b, beside, 1)
        to_core(b, beside)
        for d in range(1, highs):
            f = 2 * across(d) + low
            arrived(b, f)
            if e % 2 == 1:
                to_beside(b, f)
            to_core(b, f)

    def finish(e):
        b = origin(e)
        for d in range(1, highs):
            f = 2 * across(d) + 1 - low
            arrived(b, f)
            to_core(b, f)

    for d in range(1, band_count):
        ref = grids.at[sub_at, band_at, facet_at]
        send(ref, ref, s4.at[d - 1], r4.at[d - 1], band=lax.rem(band_at + d, band_count))

    def gather(sub, b, fresh):
        s = sub * band_count + b
        block = flat(grids[sub, b])
        if fresh:
            by_cos[...] = nt(cos_tab[s], block)
            by_sin[...] = nt(sin_tab[s], block)
        else:
            by_cos[...] += nt(cos_tab[s], block)
            by_sin[...] += nt(sin_tab[s], block)

    def gather_other(e):
        b = origin(e)
        for d in range(1, sub_count):
            other = lax.rem(sub_at + d, sub_count)
            for f in range(facet_count):
                ref = grids.at[other, b, f]
                remote(ref, ref, s6.at[d - 1, b, f], r6.at[d - 1, b, f], sub=other).wait_recv()
            gather(other, b, False)

    order = [d for pair in zip(range(1, band_count), range(band_count - 1, 0, -1)) for d in pair]
    order = [0] + list(dict.fromkeys(order))
    fan(order[0])
    for before, e in zip(order, order[1:]):
        fan(e)
        forward(before)
    finish(order[0])
    gather(sub_at, origin(order[0]), True)
    forward(order[-1])
    for before, e in zip(order, order[1:]):
        if e != order[1]:
            gather(sub_at, origin(before), False)
        finish(e)
        gather_other(before)
    gather(sub_at, origin(order[-1]), False)
    gather_other(order[-1])
    real = (by_cos[:, :contrib] - by_sin[:, contrib:]) * back_scale
    imag = (by_cos[:, contrib:] + by_sin[:, :contrib]) * back_scale
    out[:, :contrib] = real.astype(BF16)
    out[:, contrib:] = (-imag).astype(BF16)
    for copy in started:
        copy.wait_send()


def image_kernel(both, table, taper, out):
    scale = 1.0 / math.sqrt(both.shape[1] // 2)
    wide = out.shape[1]
    here = pl.ds(pl.multiple_of(pl.program_id(0) * wide, wide), wide)
    out[...] = (taper[:, here] * scale * nn(both[...], table[:, here])).astype(BF16)


def body(sizes, facets, window, facet_offsets, row_offsets, column_offset, kernel, tile_counts):
    facet_count, band_count, sub_count = sizes
    rows, width = facets.shape
    contrib = kernel.shape[0]
    subgrids = row_offsets.shape[0]
    piece = 2 * contrib // facet_count
    highs = facet_count // 2
    more = max(highs - 1, 1)
    smem = pl.BlockSpec(memory_space=pltpu.SMEM)
    vmem = pl.BlockSpec(memory_space=pltpu.VMEM)
    anywhere = pl.BlockSpec(memory_space=pl.ANY)
    taper = window.reshape(1, width)
    dma = pltpu.SemaphoreType.DMA

    def buffer(*shape, dtype=BF16):
        return pltpu.VMEM(shape, dtype)

    both, table = pl.pallas_call(
        exchange_kernel,
        out_shape=(
            pltpu.VMEM((rows, 2 * contrib), BF16),
            pltpu.VMEM((2 * contrib, width), BF16),
        ),
        in_specs=[smem, smem, smem, anywhere, vmem, vmem, vmem],
        out_specs=(vmem, vmem),
        scratch_shapes=[
            buffer(rows, width),
            buffer(2 * contrib, width),
            buffer(2 * contrib, 2 * rows),
            buffer(subgrids, rows, contrib),
            buffer(subgrids, rows, contrib),
            buffer(contrib, contrib),
            buffer(band_count, facet_count, piece, contrib),
            buffer(band_count, highs, piece, contrib),
            buffer(band_count, more, piece, contrib),
            buffer(band_count, more, 2, piece, contrib),
            buffer(band_count, piece, contrib),
            buffer(band_count, more, piece, contrib),
            buffer(band_count, piece, contrib),
            buffer(band_count - 1, piece, contrib),
            buffer(band_count - 1, piece, contrib),
            buffer(highs, piece, contrib),
            buffer(sub_count, band_count, facet_count, piece, contrib),
            buffer(rows, 2 * contrib, dtype=F32),
            buffer(rows, 2 * contrib, dtype=F32),
            dma,
        ]
        + [dma((band_count, highs))] * 2
        + [dma((band_count, more))] * 4
        + [dma((band_count,))] * 2
        + [dma((band_count - 1,))] * 2
        + [dma((more,))] * 2
        + [dma((band_count - 1,))] * 2
        + [
            dma((band_count, facet_count)),
            dma((2, band_count, more)),
            dma((band_count, facet_count)),
        ]
        + [dma((max(sub_count - 1, 1), band_count, facet_count))] * 2,
        compiler_params=pltpu.CompilerParams(
            collective_id=0, has_side_effects=True
        ),
        name="exchange",
    )(facet_offsets.T, row_offsets, column_offset, facets, taper, kernel, tile_counts)
    wide = min(width, 512)
    both = pltpu.with_memory_space_constraint(both, pltpu.VMEM)
    table = pltpu.with_memory_space_constraint(table, pltpu.VMEM)
    return pl.pallas_call(
        image_kernel,
        grid=(width // wide,),
        out_shape=jax.ShapeDtypeStruct((rows, width), BF16),
        in_specs=[vmem, vmem, vmem],
        out_specs=pl.BlockSpec((rows, wide), lambda i: (0, i)),
        compiler_params=pltpu.CompilerParams(vmem_limit_bytes=16 << 20),
        name="image",
    )(both, table, taper)


def solution(mesh):
    sizes = tuple(mesh.shape[axis] for axis in ("facet", "band", "sub"))
    in_specs = (P(("facet", "band"), None), P(), P(), P(), P(), P(), P())
    out_specs = P(("facet", "band"), None)
    return jax.shard_map(
        functools.partial(body, sizes), mesh=mesh, in_specs=in_specs, out_specs=out_specs, check_vma=False
    )
```
